32 devices in a mesh: shot: 2 (over y), gx: 8 (over z, x), gy: 2 (over core).
Axes of the slice: x: 2, y: 2, z: 4, core: 2. Of those that a mesh axis runs over, the one named last changes fastest.
Arguments:
- fields_now: float32 [4, 64, 256, 128], P('shot', 'gx', 'gy'), parts along dimension 0, may hold values from -6 to 6
- fields_later: float32 [4, 64, 256, 128], P('shot', 'gx', 'gy'), parts along dimension 0, may hold values from -6 to 6
- velocity_term: float32 [64, 256, 128], P('gx', 'gy'), may hold values from 0.05 to 0.3
- damping: float32 [64, 256, 128], P('gx', 'gy'), may hold values from 0.005 to 0.3
- traces: float32 [6, 64, 256], P('shot', 'gx', 'gy'), parts along dimension 0, may hold values from -6 to 6
- receiver_live: int32 [64, 256], P('gx', 'gy'), may hold values from 0 to 1
Outputs:
- image_sum: float32 [34, 64, 256, 128], P('shot', 'gx', 'gy'), parts along dimension 0
The draws below stay inside these ranges and needn't reach their ends.
There are 2 independent parts, one for each index of `shot`. The reference program is written for one: setup_inputs(seed, part) draws one part's arguments, and reference() takes and returns one part's arrays. A program takes and returns all parts, laid end to end along the dimension named above; an argument that names none is the same for every part. Nothing has to cross between parts.
All inputs are finite; a program needn't handle non-finite values.
Results may differ from the reference program's by a relative error of at most 0.00002.
Values sent between devices are 32-bit elements; how exact they have to be, the bound alone decides.
No kernel may reach another device: no remote copies, remote signals or barrier semaphores. Data moves between devices by JAX's collectives and lax.ppermute only.
A program may use at most 128 MiB of HBM per device.

```python
import math
import jax
import jax.numpy as jnp

NZ = 128
STEPS = 4
LAG_HALF = 8
NX = 64
NY = 256


def with_ends(drawn, key, least, top_value):
    shape = drawn.shape
    place = [jax.random.randint(jax.random.fold_in(key, axis), (), 0, shape[axis]) for axis in range(len(shape))]
    drawn = drawn.at[tuple(place)].set(least)
    longest = shape.index(max(shape))
    place[longest] = (place[longest] + 1) % shape[longest]
    return drawn.at[tuple(place)].set(top_value)


def levels(key, shape, split, least, high):
    def one(dim, parts):
        draws = jax.random.uniform(jax.random.fold_in(jax.random.fold_in(key, 6), dim), (parts,), jnp.float32, least / len(split), high / len(split))
        return jnp.repeat(jnp.exp(draws), shape[dim] // parts).reshape((-1,) + (1,) * (len(shape) - dim - 1))

    factor_of = one(*split[0])
    for cut in split[1:]:
        factor_of = factor_of * one(*cut)
    return factor_of


def centred(rng, dims, width, bound, cuts=(), dtype=jnp.bfloat16):
    result = width * jax.random.normal(rng, dims, jnp.float32)
    if cuts:
        result = result * levels(rng, dims, cuts, -0.22, 0.18)
    return jnp.clip(result, -bound, bound).astype(dtype)


def setup_inputs(seed: int = 0, part: int = 0) -> dict:
    key_of = jax.random.split(jax.random.key(seed), 7)
    part_keys = jax.random.split(jax.random.fold_in(key_of[6], part), 7)
    fields_now = centred(part_keys[0], (2, NX, NY, NZ), 1.0, 6.0, ((1, 8), (2, 2)), jnp.float32)
    fields_later = centred(part_keys[1], (2, NX, NY, NZ), 1.0, 6.0, ((1, 8), (2, 2)), jnp.float32)
    velocity_term = jnp.clip(jnp.exp(math.log(0.3) - 1.7917595 * jax.random.uniform(key_of[2], (NX, NY, NZ), jnp.float32) ** levels(key_of[2], (NX, NY, NZ), ((0, 8), (1, 2)), -0.2, 0.2)), 0.05, 0.3)
    damping = jnp.clip(jnp.exp(math.log(0.3) - 4.0943446 * jax.random.uniform(key_of[3], (NX, NY, NZ), jnp.float32) ** levels(key_of[3], (NX, NY, NZ), ((0, 8), (1, 2)), -0.2, 0.2)), 0.005, 0.3)
    traces = centred(part_keys[4], (STEPS - 1, NX, NY), 1.0, 6.0, ((1, 8), (2, 2)), jnp.float32)
    receiver_live = with_ends(jax.random.randint(key_of[5], (NX, NY), 0, 2), jax.random.fold_in(key_of[5], 1), 0, 1).astype(jnp.int32)
    return {"fields_now": fields_now, "fields_later": fields_later, "velocity_term": velocity_term, "damping": damping, "traces": traces, "receiver_live": receiver_live}


def laplacian(wavefield):
    padded = jnp.pad(wavefield, 1)
    beside_all = padded[2:, 1:-1, 1:-1] + padded[:-2, 1:-1, 1:-1]
    beside_all = beside_all + padded[1:-1, 2:, 1:-1] + padded[1:-1, :-2, 1:-1]
    beside_all = beside_all + padded[1:-1, 1:-1, 2:] + padded[1:-1, 1:-1, :-2]
    return beside_all - 6.0 * wavefield


def reference(fields_now, fields_later, velocity_term, damping, traces, receiver_live):
    current = fields_now
    following = fields_later
    live_mask = receiver_live.astype(jnp.float32)
    image_sum = jnp.zeros((2 * LAG_HALF + 1, NX, NY, NZ), jnp.float32)
    for time_step in range(STEPS):
        padded = jnp.pad(current, ((0, 0), (LAG_HALF, LAG_HALF), (0, 0), (0, 0)))
        products = []
        for offset in range(-LAG_HALF, LAG_HALF + 1):
            left = padded[0, LAG_HALF - offset:LAG_HALF - offset + NX]
            right = padded[1, LAG_HALF + offset:LAG_HALF + offset + NX]
            products.append(left * right)
        image_sum = image_sum + jnp.stack(products)
        if time_step < STEPS - 1:
            operated = jnp.stack([laplacian(current[0]), laplacian(current[1])])
            operated = operated.at[1, :, :, 0].add(live_mask * traces[time_step])
            earlier = (2.0 * current - (1.0 - damping) * following + velocity_term * operated) / (1.0 + damping)
            following = current
            current = earlier
    return image_sum
```

```python
import functools
import jax
import jax.numpy as jnp
from jax import lax
from jax.experimental import pallas as pl
from jax.experimental.pallas import tpu as pltpu
from jax.sharding import PartitionSpec as P

STEPS = 4
LAG_HALF = 8
CHUNKS = (48, 48, 32)


def padded(cells, sides, width):
    for axis, dim in sides:
        count = lax.axis_size(axis)
        ends = count - 1
        head = lax.slice_in_dim(cells, 0, width, axis=dim)
        tail = lax.slice_in_dim(cells, cells.shape[dim] - width, cells.shape[dim], axis=dim)
        cells = jnp.concatenate(
            [
                lax.ppermute(tail, axis, [(i, (i + 1) % count) for i in range(ends)]),
                cells,
                lax.ppermute(head, axis, [((i + 1) % count, i) for i in range(ends)]),
            ],
            axis=dim,
        )
    return cells


def lag_products(image_lags, slab, start, cells_x):
    updated = []
    for index, offset in enumerate(range(-LAG_HALF, LAG_HALF + 1)):
        left = slab[0, start - offset : start - offset + cells_x]
        right = slab[1, start + offset : start + offset + cells_x]
        updated.append(image_lags[index] + left * right)
    return updated


def source_mask(shape):
    channel_pick = (lax.broadcasted_iota(jnp.int32, shape, 0) == 1).astype(jnp.float32)
    surface = (lax.broadcasted_iota(jnp.int32, shape, 3) == 0).astype(jnp.float32)
    return channel_pick * surface


def plain(fields_now, fields_later, velocity_term, damping, traces, receiver_live):
    cells_x = fields_now.shape[1]
    live_mask = receiver_live.astype(jnp.float32)
    image_lags = [
        jnp.zeros(fields_now.shape[1:], jnp.float32) for offset in range(2 * LAG_HALF + 1)
    ]
    current = fields_now
    following = fields_later
    inject = source_mask(fields_now.shape)
    for time_step in range(STEPS):
        extended = padded(current, (("gx", 1),), LAG_HALF)
        image_lags = lag_products(image_lags, extended, LAG_HALF, cells_x)
        if time_step < STEPS - 1:
            crossed = padded(current, (("gy", 2),), 1)
            sum_x = (
                extended[:, LAG_HALF + 1 : LAG_HALF + 1 + cells_x]
                + extended[:, LAG_HALF - 1 : LAG_HALF - 1 + cells_x]
            )
            sum_y = crossed[:, :, 2:] + crossed[:, :, :-2]
            depth_pad = jnp.pad(current, ((0, 0), (0, 0), (0, 0), (1, 1)))
            sum_z = depth_pad[:, :, :, 2:] + depth_pad[:, :, :, :-2]
            source_plane = (live_mask * traces[time_step])[None, :, :, None]
            operated = sum_x + sum_y + sum_z - 6.0 * current + inject * source_plane
            earlier = (2.0 * current - (1.0 - damping) * following + velocity_term * operated) / (
                1.0 + damping
            )
            following = current
            current = earlier
    return jnp.stack(image_lags)


X = 8
Y = 128
Z = 128
G = 8
F32 = jnp.float32
HBM = pl.BlockSpec(memory_space=pltpu.HBM)
VMEM = pl.BlockSpec(memory_space=pltpu.VMEM)


def by8(value):
    return pl.multiple_of(value, G)


def place():
    even = lax.axis_index("gx") % 2 == 0
    return even, lax.axis_index("gy"), lax.axis_index("shot")


def run_copies(pieces, sem):
    copies = [pltpu.make_async_copy(a, b, sem.at[j]) for j, (a, b) in enumerate(pieces)]
    for c in copies:
        c.start()
    return copies


def wait_all(copies):
    for c in copies:
        c.wait()


def shifted(ref, f, row, lo, size, first, last):
    centre = ref[f, row, lo : lo + size]
    total = ref[f, row - 1, lo : lo + size] + ref[f, row + 1, lo : lo + size]
    total += ref[f, row, lo - 1 : lo - 1 + size] + ref[f, row, lo + 1 : lo + 1 + size]
    total += jnp.where(first, 0.0, pltpu.roll(centre, 1, 1))
    total += jnp.where(last, 0.0, pltpu.roll(centre, Z - 1, 1))
    return centre, total


def coefficients(vel, damp):
    inv = 1.0 / (1.0 + damp)
    gain = vel * inv
    return (1.0 - damp) * inv, gain, 2.0 * inv - 6.0 * gain


def prep_kernel(u0, v, d, traces, live, edge, rest, mine, on0, brink, t, sem):
    even, gy, shot = place()
    row = jnp.where(even, X - 1, 0)
    y = by8(jnp.where(gy == 0, Y - G, 0))
    for n in range(2):
        t[n] = live[...].astype(F32) * traces[n + 1]
    own = pl.ds(0, Y)
    pieces = [
        (u0.at[:, 0], edge.at[:, 0, own]),
        (u0.at[:, X - 1], edge.at[:, 1, own]),
        (t.at[0], edge.at[0, 0, pl.ds(Y, G)]),
        (t.at[1], edge.at[0, 1, pl.ds(Y, G)]),
        (u0.at[:, :, pl.ds(y, G)], brink),
        (u0.at[:, row], on0.at[pl.ds(0, 2), own]),
        (v.at[row], on0.at[2, own]),
        (d.at[row], on0.at[3, own]),
        (t.at[0], on0.at[0, pl.ds(Y, G)]),
        (t.at[1], on0.at[1, pl.ds(Y, G)]),
        (u0.at[:, pl.ds(1, 6)], rest),
    ]
    copies = run_copies(pieces, sem)

    @pl.when(shot == 0)
    def _():
        pltpu.make_async_copy(v, mine, sem.at[len(pieces)]).start()

    @pl.when(shot != 0)
    def _():
        pltpu.make_async_copy(d, mine, sem.at[len(pieces)]).start()

    wait_all(copies)
    pltpu.make_async_copy(v, mine, sem.at[len(pieces)]).wait()


def surface_columns(rows):
    wide = jnp.concatenate([rows, jnp.zeros((Z - rows.shape[0], Y), F32)], 0)
    return wide.T


def first_kernel(chunks, *args):
    u0, later, v, d, near_e, far_e, beside, traces, live = args[:9]
    u1, on1, back = args[9:12]
    parts = args[12 : 12 + len(chunks)]
    c, f0, vel, damp, out, t, sem = args[12 + len(chunks) :]
    even, gy, shot = place()
    own = pl.ds(0, Y)
    near_pick, near_row = jnp.where(even, 0, 1), jnp.where(even, 9, 0)
    far_pick, far_row = jnp.where(even, 1, 0), jnp.where(even, 0, 9)
    mid = pl.ds(G, Y)
    at = by8(jnp.where(gy == 0, Y + G, 0))
    copies = run_copies(
        [
            (u0, c.at[:, pl.ds(1, X), mid]),
            (near_e.at[:, near_pick, own], c.at[:, near_row, mid]),
            (far_e.at[:, far_pick, own], c.at[:, far_row, mid]),
            (beside, c.at[:, pl.ds(1, X), pl.ds(at, G)]),
            (later, f0),
            (v, vel),
            (d, damp),
        ],
        sem,
    )
    rim = by8(jnp.where(gy == 0, 0, Y + G))
    for f in range(2):
        for x in range(X):
            c[f, x + 1, pl.ds(rim, G)] = jnp.zeros((G, Z), F32)
    mask = live[...].astype(F32)
    for n in range(2):
        t[n] = mask * traces[n + 1]
    column = surface_columns(mask * traces[0])
    wait_all(copies)
    row = jnp.where(even, 0, X - 1)
    early = run_copies(
        [
            (c.at[:, row + 1, mid], back.at[pl.ds(0, 2), own]),
            (vel.at[row], back.at[2, own]),
            (damp.at[row], back.at[3, own]),
            (t.at[0], back.at[0, pl.ds(Y, G)]),
            (t.at[1], back.at[1, pl.ds(Y, G)]),
        ],
        sem,
    )
    lane = lax.broadcasted_iota(jnp.int32, (Y, Z), 1)
    first, last = lane == 0, lane == Z - 1
    for x in range(X):
        pull, gain, keep = coefficients(vel[x], damp[x])
        for f in range(2):
            centre, total = shifted(c, f, x + 1, G, Y, first, last)
            if f == 1:
                turned = pltpu.roll(column, Z - x, 1) if x else column
                total += jnp.where(first, turned, 0.0)
            out[f, x] = keep * centre - pull * f0[f, x] + gain * total
    wait_all(early)
    away = pl.ds(jnp.where(even, 6, 0), 2)
    toward = jnp.where(even, 0, 6)
    pieces = [(out, u1), (out.at[:, away], on1)]
    for f in range(2):
        pieces.append((out.at[f, pl.ds(toward, 2)], back.at[pl.ds(4 + 2 * f, 2), own]))
    begin = 0
    for width, part in zip(chunks, parts):
        y = by8(jnp.where(gy == 1, begin, Y - begin - width))
        pieces.append((out.at[:, :, pl.ds(y, width)], part))
        begin += width
    wait_all(run_copies(pieces, sem))


NAMES0 = ("ne", "nr", "na", "nb", "fe", "fr", "fa", "fb", "u0", "v", "d", "on", "back")
NAMES1 = ("u1", "on1")


def level0_pieces(refs, u0, co, src, dst, size, even, shot):
    near, far = jnp.where(even, 17, 1), jnp.where(even, 1, 17)
    s, d = pl.ds(src, size), pl.ds(dst, size)
    out = []
    for base, edge, rest, mine, other in (
        (near, refs["ne"], refs["nr"], refs["na"], refs["nb"]),
        (far, refs["fe"], refs["fr"], refs["fa"], refs["fb"]),
    ):
        out.append((edge.at[:, 0, s], u0(base, None, d)))
        out.append((edge.at[:, 1, s], u0(base + 7, None, d)))
        out.append((rest.at[:, :, s], u0(base + 1, 6, d)))
        out.append((mine.at[:, s], co(base, X, d, shot)))
        out.append((other.at[:, s], co(base, X, d, 1 - shot)))
    out.append((refs["u0"].at[:, :, s], u0(9, X, d)))
    out.append((refs["v"].at[:, s], co(9, X, d, 0)))
    out.append((refs["d"].at[:, s], co(9, X, d, 1)))
    for row, part in ((jnp.where(even, 0, 25), refs["on"]), (jnp.where(even, 25, 0), refs["back"])):
        out.append((part.at[pl.ds(0, 2), s], u0(row, None, d)))
        out.append((part.at[pl.ds(2, 2), s], co(row, None, d, None)))
    return out


def target(ref):
    def pick(row, rows, d, lead=None):
        lead = slice(None) if lead is None else lead
        return ref.at[lead, row if rows is None else pl.ds(row, rows), d]

    return pick


def level1_own(refs, u1, src, dst, size, even):
    s, d = pl.ds(src, size), pl.ds(dst, size)
    on, back = jnp.where(even, 0, 26), jnp.where(even, 26, 0)
    out = [
        (refs["u1"].at[:, :, s], u1.at[:, pl.ds(10, X), d]),
        (refs["on1"].at[:, :, s], u1.at[:, pl.ds(on, 2), d]),
    ]
    for f in range(2):
        out.append((refs["back"].at[pl.ds(4 + 2 * f, 2), s], u1.at[f, pl.ds(back, 2), d]))
    return out


def level1_chunk(near_ref, far_ref, u1, src, dst, size, even):
    near, far = jnp.where(even, 18, 2), jnp.where(even, 2, 18)
    s, d = pl.ds(src, size), pl.ds(dst, size)
    return [
        (near_ref.at[:, :, s], u1.at[:, pl.ds(near, X), d]),
        (far_ref.at[:, :, s], u1.at[:, pl.ds(far, X), d]),
    ]


def rim0_kernel(*args):
    refs = dict(zip(NAMES0, args))
    traces, live, rim, columns, rows, u0, co, sem = args[len(NAMES0) :]
    even, gy, shot = place()
    y = by8(jnp.where(gy == 0, Y - G, 0))
    pieces = level0_pieces(refs, target(u0), target(co), y, 0, G, even, shot)
    for part, at in (
        (refs["ne"], jnp.where(even, 24, 8)),
        (refs["fe"], jnp.where(even, 8, 24)),
        (refs["on"], jnp.where(even, 0, 32)),
        (refs["back"], jnp.where(even, 32, 0)),
    ):
        for n in range(2):
            spot = part.at[0, n] if len(part.shape) == 4 else part.at[n]
            pieces.append((spot.at[pl.ds(Y, G)], rows.at[n, pl.ds(by8(at), X)]))
    copies = run_copies(pieces, sem)
    mask = live[...].astype(F32)
    for n in range(2):
        rows[n, 16:24] = mask * traces[n + 1]
    wait_all(copies)
    for f in range(2):
        rim[26 * f : 26 * f + 26] = u0[f]
        rim[52 + 26 * f : 78 + 26 * f] = co[f]
    for n in range(2):
        columns[n] = surface_columns(rows[n])
        rim[104 + n] = columns[n, pl.ds(y, G)]


def rim1_kernel(chunk, *args):
    refs = dict(zip(("u1", "on1", "back"), args))
    near, far, out, sem = args[3:]
    even, gy, shot = place()
    y = by8(jnp.where(gy == 0, Y - G, 0))
    yc = by8(jnp.where(gy == 0, chunk - G, 0))
    pieces = level1_own(refs, out, y, 0, G, even) + level1_chunk(near, far, out, yc, 0, G, even)
    wait_all(run_copies(pieces, sem))


def slab_kernel(k, chunks, *args):
    n_in = len(NAMES0) + len(NAMES1)
    refs = dict(zip(NAMES0 + NAMES1, args[:n_in]))
    rest = list(args[n_in:])
    columns = rest.pop(0)
    near_k, far_k = rest.pop(0), rest.pop(0)
    first_slab, last_slab = k == 0, k == len(chunks) - 1
    if first_slab:
        rim0, rim1 = rest.pop(0), rest.pop(0)
    else:
        near_p, far_p, _ = rest.pop(0), rest.pop(0), rest.pop(0)
    out_hbm, u0, u1, u2, u3, co, abc, inj, image, sem, out_sem = rest
    even, gy, shot = place()
    start, width = sum(chunks[:k]), chunks[k]
    lead = G if first_slab else 2 * G
    span = lead + width + (G if last_slab else 0)
    size = span - 2 * G

    def spot(at, length, total):
        return by8(jnp.where(gy == 1, at, total - at - length))

    ahead = 0 if first_slab else 2 * G
    src = spot(start - ahead, ahead + width, Y)
    here = spot(lead - ahead, ahead + width, span)
    dst = by8(here + G)
    pieces = level0_pieces(refs, target(u0), target(co), src, dst, ahead + width, even, shot)
    pieces += level1_own(refs, u1, src, dst, ahead + width, even)
    pieces.append((columns.at[:, pl.ds(src, ahead + width)], inj.at[:, pl.ds(here, ahead + width)]))
    at = by8(spot(lead, width, span) + G)
    pieces += level1_chunk(near_k, far_k, u1, 0, at, width, even)
    if first_slab:
        at = by8(spot(0, G, span) + G)
        pieces.append((rim1, u1.at[:, :, pl.ds(at, G)]))
        for f in range(2):
            pieces.append((rim0.at[pl.ds(26 * f, 26)], u0.at[f, :, pl.ds(at, G)]))
            pieces.append((rim0.at[pl.ds(52 + 26 * f, 26)], co.at[f, :, pl.ds(at, G)]))
        pieces.append((rim0.at[pl.ds(104, 2)], inj.at[:, pl.ds(by8(spot(0, G, span)), G)]))
    else:
        before = chunks[k - 1]
        at = by8(spot(0, 2 * G, span) + G)
        pieces += level1_chunk(
            near_p, far_p, u1, spot(before - 2 * G, 2 * G, before), at, 2 * G, even
        )
    copies = run_copies(pieces, sem)
    if last_slab:
        edge = spot(span - G, G, span)
        for ref in (u0, u1, co):
            for j in range(ref.shape[1]):
                ref[:, j, pl.ds(by8(edge + G), G)] = jnp.zeros((2, G, Z), F32)
        inj[:, pl.ds(edge, G)] = jnp.zeros((2, G, Z), F32)
    wait_all(copies)

    lane = lax.broadcasted_iota(jnp.int32, (span, Z), 1)
    first, last = lane == 0, lane == Z - 1
    y = slice(G, G + span)

    def second(row, carry):
        pull, gain, keep = coefficients(co[0, row, y], co[1, row, y])
        abc[0, row, y] = pull
        abc[1, row, y] = gain
        abc[2, row, y] = keep
        for f in range(2):
            centre, total = shifted(u1, f, row + 1, G, span, first, last)
            if f == 1:
                total += jnp.where(first, pltpu.roll(inj[0], 121 - row, 1), 0.0)
            u2[f, row, y] = keep * centre - pull * u0[f, row, y] + gain * total
        return carry

    lax.fori_loop(0, 26, second, 0, unroll=13)
    first_, last_ = first[:size], last[:size]
    yy = slice(2 * G, 2 * G + size)

    def third(row, carry):
        for f in range(2):
            centre, total = shifted(u2, f, row + 1, 2 * G, size, first_, last_)
            if f == 1:
                total += jnp.where(first_, pltpu.roll(inj[1, G : G + size], 120 - row, 1), 0.0)
            u3[f, row, yy] = (
                abc[2, row + 1, yy] * centre
                - abc[0, row + 1, yy] * u1[f, row + 2, yy]
                + abc[1, row + 1, yy] * total
            )
        return carry

    lax.fori_loop(0, 24, third, 0, unroll=12)
    levels = ((u0, 9), (u1, 10), (u2, 9), (u3, 8))
    groups = size // G
    low = spot((start if first_slab else start - G), size, Y)

    def out_copy(g):
        return pltpu.make_async_copy(
            image.at[:, :, pl.ds(by8(g * G), G)],
            out_hbm.at[:, :, pl.ds(by8(low + g * G), G)],
            out_sem.at[g],
        )

    def products(g, carry):
        cells = pl.ds(by8(2 * G + g * G), G)
        for parity in range(2):
            for tile in range(3):
                rows_a = [-8 + parity + 8 * tile + 2 * j for j in range(4)]
                held = [[ref[0, a + o, cells] for ref, o in levels] for a in rows_a]
                for b in range(-8 + parity, 16, 2):
                    wanted = [
                        j for j, a in enumerate(rows_a) if 0 <= a + b < 16 and abs(b - a) <= 16
                    ]
                    if not wanted:
                        continue
                    right = [ref[1, b + o, cells] for ref, o in levels]
                    for j in wanted:
                        a = rows_a[j]
                        p = [l * r for l, r in zip(held[j], right)]
                        image[(b - a) // 2 + 8, (a + b) // 2, pl.ds(by8(g * G), G)] = (
                            p[0] + p[1]
                        ) + (p[2] + p[3])
        out_copy(g).start()
        return carry

    lax.fori_loop(0, groups, products, 0)
    for g in range(groups):
        out_copy(g).wait()


def call(kernel, outs, args, specs, scratch, name, out_specs=None, **extra):
    return pl.pallas_call(
        kernel,
        out_shape=[jax.ShapeDtypeStruct(s, F32) for s in outs],
        in_specs=specs,
        out_specs=out_specs or [HBM] * len(outs),
        scratch_shapes=scratch,
        compiler_params=pltpu.CompilerParams(vmem_limit_bytes=48 << 20),
        name=name,
        **extra,
    )(*args)


def shards(fields_now, fields_later, velocity_term, damping, traces, receiver_live):
    count = lax.axis_size("gx")
    swap_x = [(i, i ^ 1) for i in range(count)]
    onward = [(i, i + 2) for i in range(0, count - 2, 2)]
    onward += [(i, i - 2) for i in range(3, count, 2)]
    backward = [(b, a) for a, b in onward]
    swap = [(0, 1), (1, 0)]
    dma = pltpu.SemaphoreType.DMA
    vm = pltpu.VMEM
    u0 = fields_now
    small = [VMEM, VMEM]

    edge, rest, mine, on0, brink = call(
        prep_kernel,
        [(2, 2, Y + G, Z), (2, 6, Y, Z), (X, Y, Z), (4, Y + G, Z), (2, X, G, Z)],
        (u0, velocity_term, damping, traces, receiver_live),
        [HBM] * 3 + small,
        [vm((2, X, Y), F32), dma((12,))],
        "prep",
    )
    near_edge = lax.ppermute(edge, "gx", swap_x)
    beside = lax.ppermute(brink, "gy", swap)
    near_mine = lax.ppermute(mine, "gx", swap_x)
    near_rest = lax.ppermute(rest, "gx", swap_x)
    from_on0 = lax.ppermute(on0, "gx", onward)
    far_edge = lax.ppermute(near_edge, "gx", onward)

    u1, on1, back, *parts = call(
        functools.partial(first_kernel, CHUNKS),
        [(2, X, Y, Z), (2, 2, Y, Z), (8, Y + G, Z)] + [(2, X, w, Z) for w in CHUNKS],
        (u0, fields_later, velocity_term, damping, near_edge, far_edge, beside, traces,
         receiver_live),
        [HBM] * 7 + small,
        [
            vm((2, X + 2, Y + 2 * G, Z), F32),
            vm((2, X, Y, Z), F32),
            vm((X, Y, Z), F32),
            vm((X, Y, Z), F32),
            vm((2, X, Y, Z), F32),
            vm((2, X, Y), F32),
            dma((7 + len(CHUNKS),)),
        ],
        "first",
    )
    near_chunks = [lax.ppermute(p, "gx", swap_x) for p in parts]
    from_back = lax.ppermute(back, "gx", backward)
    from_on1 = lax.ppermute(on1, "gx", onward)
    far_mine = lax.ppermute(near_mine, "gx", onward)
    near_other = lax.ppermute(near_mine, "shot", swap)
    far_other = lax.ppermute(far_mine, "shot", swap)
    far_rest = lax.ppermute(near_rest, "gx", onward)
    far_chunks = [lax.ppermute(c, "gx", onward) for c in near_chunks]

    base0 = (
        near_edge, near_rest, near_mine, near_other,
        far_edge, far_rest, far_mine, far_other,
        u0, velocity_term, damping, from_on0, from_back,
    )
    base1 = (u1, from_on1)
    rim0, columns = call(
        rim0_kernel,
        [(106, G, Z), (2, Y, Z)],
        (*base0, traces, receiver_live),
        [HBM] * len(base0) + small,
        [vm((2, 40, Y), F32), vm((2, 26, G, Z), F32), vm((2, 26, G, Z), F32), dma((25,))],
        "rim0",
        [VMEM, VMEM],
    )
    rim0 = lax.ppermute(rim0, "gy", swap)
    (rim1,) = call(
        functools.partial(rim1_kernel, CHUNKS[0]),
        [(2, 28, G, Z)],
        (*base1, from_back, near_chunks[0], far_chunks[0]),
        [HBM] * 5,
        [dma((6,))],
        "rim1",
        [VMEM],
    )
    rim1 = lax.ppermute(rim1, "gy", swap)

    image = None
    for k, width in enumerate(CHUNKS):
        first_slab, last_slab = k == 0, k == len(CHUNKS) - 1
        span = (G if first_slab else 2 * G) + width + (G if last_slab else 0)
        args = [*base0, *base1, columns, near_chunks[k], far_chunks[k]]
        if first_slab:
            args += [rim0, rim1]
        else:
            args += [near_chunks[k - 1], far_chunks[k - 1], image]
        wide = span + 2 * G
        (image,) = call(
            functools.partial(slab_kernel, k, CHUNKS),
            [(2 * LAG_HALF + 1, X, Y, Z)],
            args,
            [HBM] * len(args),
            [
                vm((2, 26, wide, Z), F32),
                vm((2, 28, wide, Z), F32),
                vm((2, 26, wide, Z), F32),
                vm((2, 24, wide, Z), F32),
                vm((2, 26, wide, Z), F32),
                vm((3, 26, wide, Z), F32),
                vm((2, span, Z), F32),
                vm((2 * LAG_HALF + 1, X, span - 2 * G, Z), F32),
                dma((32,)),
                dma((max(1, (span - 2 * G) // G),)),
            ],
            f"slab{k}",
            input_output_aliases={} if first_slab else {len(args) - 1: 0},
        )
    return image


def solution(mesh):
    placed = (
        P("shot", "gx", "gy", None),
        P("shot", "gx", "gy", None),
        P("gx", "gy", None),
        P("gx", "gy", None),
        P("shot", "gx", "gy"),
        P("gx", "gy"),
    )

    def body(fields_now, *others):
        fits = fields_now.shape == (2, X, 128, 128) and mesh.shape["gx"] % 2 == 0
        fits = fits and mesh.shape["gy"] == 2 and mesh.shape["shot"] == 2
        return (shards if fits else plain)(fields_now, *others)

    return jax.shard_map(
        body, mesh=mesh, in_specs=placed, out_specs=P("shot", "gx", "gy", None), check_vma=False
    )
```

```python
import functools
import jax
import jax.numpy as jnp
from jax import lax
from jax.experimental import pallas as pl
from jax.experimental.pallas import tpu as pltpu
from jax.sharding import PartitionSpec as P

STEPS = 4
LAG_HALF = 8
CHUNKS = (64, 64)


def padded(cells, sides, width):
    for axis, dim in sides:
        count = lax.axis_size(axis)
        ends = count - 1
        head = lax.slice_in_dim(cells, 0, width, axis=dim)
        tail = lax.slice_in_dim(cells, cells.shape[dim] - width, cells.shape[dim], axis=dim)
        cells = jnp.concatenate(
            [
                lax.ppermute(tail, axis, [(i, (i + 1) % count) for i in range(ends)]),
                cells,
                lax.ppermute(head, axis, [((i + 1) % count, i) for i in range(ends)]),
            ],
            axis=dim,
        )
    return cells


def lag_products(image_lags, slab, start, cells_x):
    updated = []
    for index, offset in enumerate(range(-LAG_HALF, LAG_HALF + 1)):
        left = slab[0, start - offset : start - offset + cells_x]
        right = slab[1, start + offset : start + offset + cells_x]
        updated.append(image_lags[index] + left * right)
    return updated


def source_mask(shape):
    channel_pick = (lax.broadcasted_iota(jnp.int32, shape, 0) == 1).astype(jnp.float32)
    surface = (lax.broadcasted_iota(jnp.int32, shape, 3) == 0).astype(jnp.float32)
    return channel_pick * surface


def plain(fields_now, fields_later, velocity_term, damping, traces, receiver_live):
    cells_x = fields_now.shape[1]
    live_mask = receiver_live.astype(jnp.float32)
    image_lags = [
        jnp.zeros(fields_now.shape[1:], jnp.float32) for offset in range(2 * LAG_HALF + 1)
    ]
    current = fields_now
    following = fields_later
    inject = source_mask(fields_now.shape)
    for time_step in range(STEPS):
        extended = padded(current, (("gx", 1),), LAG_HALF)
        image_lags = lag_products(image_lags, extended, LAG_HALF, cells_x)
        if time_step < STEPS - 1:
            crossed = padded(current, (("gy", 2),), 1)
            sum_x = (
                extended[:, LAG_HALF + 1 : LAG_HALF + 1 + cells_x]
                + extended[:, LAG_HALF - 1 : LAG_HALF - 1 + cells_x]
            )
            sum_y = crossed[:, :, 2:] + crossed[:, :, :-2]
            depth_pad = jnp.pad(current, ((0, 0), (0, 0), (0, 0), (1, 1)))
            sum_z = depth_pad[:, :, :, 2:] + depth_pad[:, :, :, :-2]
            source_plane = (live_mask * traces[time_step])[None, :, :, None]
            operated = sum_x + sum_y + sum_z - 6.0 * current + inject * source_plane
            earlier = (2.0 * current - (1.0 - damping) * following + velocity_term * operated) / (
                1.0 + damping
            )
            following = current
            current = earlier
    return jnp.stack(image_lags)


PARTS = 5
X = 8
Y = 128
Z = 128
G = 8
F32 = jnp.float32
HBM = pl.BlockSpec(memory_space=pltpu.HBM)
VMEM = pl.BlockSpec(memory_space=pltpu.VMEM)


def by8(value):
    return pl.multiple_of(value, G)


def place():
    even = lax.axis_index("gx") % 2 == 0
    return even, lax.axis_index("gy"), lax.axis_index("shot")


def run_copies(pieces, sem):
    copies = [pltpu.make_async_copy(a, b, sem.at[j]) for j, (a, b) in enumerate(pieces)]
    for c in copies:
        c.start()
    return copies


def wait_all(copies):
    for c in copies:
        c.wait()


def shifted(ref, f, row, lo, size, first, last):
    centre = ref[f, row, lo : lo + size]
    total = ref[f, row - 1, lo : lo + size] + ref[f, row + 1, lo : lo + size]
    total += ref[f, row, lo - 1 : lo - 1 + size] + ref[f, row, lo + 1 : lo + 1 + size]
    total += jnp.where(first, 0.0, pltpu.roll(centre, 1, 1))
    total += jnp.where(last, 0.0, pltpu.roll(centre, Z - 1, 1))
    return centre, total


def coefficients(vel, damp):
    inv = 1.0 / (1.0 + damp)
    gain = vel * inv
    return (1.0 - damp) * inv, gain, 2.0 * inv - 6.0 * gain


def receivers(traces_hbm, live_hbm, traces, live, sem):
    copies = run_copies([(traces_hbm, traces), (live_hbm, live)], sem)
    wait_all(copies)
    return live[...].astype(F32)


def edge_kernel(u0, edge, brink, sem):
    even, gy, shot = place()
    y = by8(jnp.where(gy == 0, Y - G, 0))
    pieces = [(u0.at[:, r], edge.at[:, e]) for e, r in ((0, 0), (1, X - 1))]
    pieces.append((u0.at[:, :, pl.ds(y, G)], brink))
    wait_all(run_copies(pieces, sem))


def prep_kernel(u0, v, d, traces_hbm, live_hbm, mine, rest, on0, back0, *scratch):
    t, traces, live, sem, sem2 = scratch
    even, gy, shot = place()
    own = pl.ds(0, Y)
    row = jnp.where(even, X - 1, 0)

    @pl.when(shot == 0)
    def _():
        pltpu.make_async_copy(v, mine.at[:, own], sem.at[7]).start()

    @pl.when(shot != 0)
    def _():
        pltpu.make_async_copy(d, mine.at[:, own], sem.at[7]).start()

    pieces = [(u0.at[:, pl.ds(1, 6)], rest)]
    for part, r in ((on0, row), (back0, X - 1 - row)):
        pieces.append((u0.at[:, r], part.at[pl.ds(0, 2), own]))
        pieces.append((v.at[r], part.at[2, own]))
        pieces.append((d.at[r], part.at[3, own]))
    copies = run_copies(pieces, sem)
    mask = receivers(traces_hbm, live_hbm, traces, live, sem2)
    for n in range(2):
        t[n] = mask * traces[n + 1]
    late = []
    for n in range(2):
        for k, part in enumerate((mine, on0, back0)):
            c = pltpu.make_async_copy(t.at[n], part.at[n, pl.ds(Y, G)], sem2.at[2 + 2 * k + n])
            c.start()
            late.append(c)
    wait_all(copies + late)
    pltpu.make_async_copy(v, mine.at[:, own], sem.at[7]).wait()


def surface_columns(rows):
    wide = jnp.concatenate([rows, jnp.zeros((Z - rows.shape[0], Y), F32)], 0)
    return wide.T


def first_kernel(chunks, *args):
    u0, later, v, d, near_e, far_e, beside, traces_hbm, live_hbm = args[:9]
    u1, on1, brow = args[9:12]
    parts = args[12 : 12 + len(chunks)]
    c, f0, vel, damp, out, traces, live, sem, sem2 = args[12 + len(chunks) :]
    even, gy, shot = place()
    own = pl.ds(0, Y)
    near_pick, near_row = jnp.where(even, 0, 1), jnp.where(even, 9, 0)
    far_pick, far_row = jnp.where(even, 1, 0), jnp.where(even, 0, 9)
    mid = pl.ds(G, Y)
    at = by8(jnp.where(gy == 0, Y + G, 0))
    copies = run_copies(
        [
            (u0, c.at[:, pl.ds(1, X), mid]),
            (near_e.at[:, near_pick], c.at[:, near_row, mid]),
            (far_e.at[:, far_pick], c.at[:, far_row, mid]),
            (beside, c.at[:, pl.ds(1, X), pl.ds(at, G)]),
            (later, f0),
            (v, vel),
            (d, damp),
        ],
        sem,
    )
    rim = by8(jnp.where(gy == 0, 0, Y + G))
    for f in range(2):
        for x in range(X):
            c[f, x + 1, pl.ds(rim, G)] = jnp.zeros((G, Z), F32)
    mask = receivers(traces_hbm, live_hbm, traces, live, sem2)
    column = surface_columns(mask * traces[0])
    wait_all(copies)
    lane = lax.broadcasted_iota(jnp.int32, (Y, Z), 1)
    first, last = lane == 0, lane == Z - 1
    for x in range(X):
        pull, gain, keep = coefficients(vel[x], damp[x])
        for f in range(2):
            centre, total = shifted(c, f, x + 1, G, Y, first, last)
            if f == 1:
                turned = pltpu.roll(column, Z - x, 1) if x else column
                total += jnp.where(first, turned, 0.0)
            out[f, x] = keep * centre - pull * f0[f, x] + gain * total
    row = jnp.where(even, 0, 6)
    pieces = [(out, u1), (out.at[:, pl.ds(6 - row, 2)], on1), (out.at[:, pl.ds(row, 2)], brow)]
    others = pl.ds(jnp.where(even, 2, 0), 6)
    begin = 0
    for width, part in zip(chunks, parts):
        y = by8(jnp.where(gy == 1, begin, Y - begin - width))
        pieces.append((out.at[:, others, pl.ds(y, width)], part))
        begin += width
    wait_all(run_copies(pieces, sem))


NAMES0 = ("ne", "nr", "na", "nb", "fe", "fr", "fa", "fb", "u0", "v", "d", "on", "back")
NAMES1 = ("u1", "on1", "back1", "nw", "fw")


def level0_pieces(refs, u0, co, src, dst, size, even, shot):
    near, far = jnp.where(even, 17, 1), jnp.where(even, 1, 17)
    s, d = pl.ds(src, size), pl.ds(dst, size)
    early, late = [], []
    for out, base, edge, rest, mine, other in (
        (early, near, refs["ne"], refs["nr"], refs["na"], refs["nb"]),
        (late, far, refs["fe"], refs["fr"], refs["fa"], refs["fb"]),
    ):
        out.append((edge.at[:, 0, s], u0(base, None, d)))
        out.append((edge.at[:, 1, s], u0(base + 7, None, d)))
        out.append((rest.at[:, :, s], u0(base + 1, 6, d)))
        out.append((mine.at[:, s], co(base, X, d, shot)))
        out.append((other.at[:, s], co(base, X, d, 1 - shot)))
    early.append((refs["u0"].at[:, :, s], u0(9, X, d)))
    early.append((refs["v"].at[:, s], co(9, X, d, 0)))
    early.append((refs["d"].at[:, s], co(9, X, d, 1)))
    for row, part in ((jnp.where(even, 0, 25), refs["on"]), (jnp.where(even, 25, 0), refs["back"])):
        late.append((part.at[pl.ds(0, 2), s], u0(row, None, d)))
        late.append((part.at[pl.ds(2, 2), s], co(row, None, d, None)))
    return early, late


def target(ref):
    def pick(row, rows, d, lead=None):
        lead = slice(None) if lead is None else lead
        return ref.at[lead, row if rows is None else pl.ds(row, rows), d]

    return pick


def level1_own(refs, u1, src, dst, size, even):
    s, d = pl.ds(src, size), pl.ds(dst, size)
    early = [(refs["u1"].at[:, :, s], u1.at[:, pl.ds(10, X), d])]
    late = []
    for out, part, at_even, at_odd in (
        (early, "nw", 24, 2), (late, "fw", 8, 18), (late, "on1", 0, 26), (late, "back1", 26, 0),
    ):
        row = jnp.where(even, at_even, at_odd)
        out.append((refs[part].at[:, :, s], u1.at[:, pl.ds(row, 2), d]))
    return early, late


def level1_chunk(near_ref, far_ref, u1, src, dst, size, even):
    near, far = jnp.where(even, 18, 4), jnp.where(even, 2, 20)
    s, d = pl.ds(src, size), pl.ds(dst, size)
    return (
        [(near_ref.at[:, :, s], u1.at[:, pl.ds(near, 6), d])],
        [(far_ref.at[:, :, s], u1.at[:, pl.ds(far, 6), d])],
    )


def rim0_kernel(*args):
    refs = dict(zip(NAMES0, args))
    traces_hbm, live_hbm, rim, columns, rows, u0, co, traces, live, sem, sem2 = args[len(NAMES0) :]
    even, gy, shot = place()
    y = by8(jnp.where(gy == 0, Y - G, 0))
    early, late = level0_pieces(refs, target(u0), target(co), y, 0, G, even, shot)
    pieces = early + late
    for part, at in (
        (refs["na"], jnp.where(even, 24, 8)),
        (refs["fa"], jnp.where(even, 8, 24)),
        (refs["on"], jnp.where(even, 0, 32)),
        (refs["back"], jnp.where(even, 32, 0)),
    ):
        for n in range(2):
            pieces.append((part.at[n, pl.ds(Y, G)], rows.at[n, pl.ds(by8(at), X)]))
    copies = run_copies(pieces, sem)
    mask = receivers(traces_hbm, live_hbm, traces, live, sem2)
    for n in range(2):
        rows[n, 16:24] = mask * traces[n + 1]
    wait_all(copies)
    for f in range(2):
        rim[26 * f : 26 * f + 26] = u0[f]
        rim[52 + 26 * f : 78 + 26 * f] = co[f]
    for n in range(2):
        columns[n] = surface_columns(rows[n])
        rim[104 + n] = columns[n, pl.ds(y, G)]


def rim1_kernel(chunk, *args):
    refs = dict(zip(NAMES1, args))
    near, far, out, sem = args[len(NAMES1) :]
    even, gy, shot = place()
    y = by8(jnp.where(gy == 0, Y - G, 0))
    yc = by8(jnp.where(gy == 0, chunk - G, 0))
    pieces = level1_own(refs, out, y, 0, G, even) + level1_chunk(near, far, out, yc, 0, G, even)
    wait_all(run_copies(sum(pieces, []), sem))


def slab_kernel(k, chunks, *args):
    n_in = len(NAMES0) + len(NAMES1)
    refs = dict(zip(NAMES0 + NAMES1, args[:n_in]))
    rest = list(args[n_in:])
    columns = rest.pop(0)
    near_k, far_k = rest.pop(0), rest.pop(0)
    first_slab, last_slab = k == 0, k == len(chunks) - 1
    if first_slab:
        rim0, rim1 = rest.pop(0), rest.pop(0)
    else:
        near_p, far_p, _ = rest.pop(0), rest.pop(0), rest.pop(0)
    out_hbm, u0, u1, u2, u3, co, abc, inj, image, sem, out_sem = rest
    even, gy, shot = place()
    start, width = sum(chunks[:k]), chunks[k]
    lead = G if first_slab else 2 * G
    span = lead + width + (G if last_slab else 0)
    size = span - 2 * G

    def spot(at, length, total):
        return by8(jnp.where(gy == 1, at, total - at - length))

    ahead = 0 if first_slab else 2 * G
    src = spot(start - ahead, ahead + width, Y)
    here = spot(lead - ahead, ahead + width, span)
    dst = by8(here + G)
    batches = [
        level0_pieces(refs, target(u0), target(co), src, dst, ahead + width, even, shot),
        level1_own(refs, u1, src, dst, ahead + width, even),
    ]
    at = by8(spot(lead, width, span) + G)
    batches.append(level1_chunk(near_k, far_k, u1, 0, at, width, even))
    early = [(columns.at[:, pl.ds(src, ahead + width)], inj.at[:, pl.ds(here, ahead + width)])]
    if first_slab:
        at = by8(spot(0, G, span) + G)
        early.append((rim1, u1.at[:, :, pl.ds(at, G)]))
        for f in range(2):
            early.append((rim0.at[pl.ds(26 * f, 26)], u0.at[f, :, pl.ds(at, G)]))
            early.append((rim0.at[pl.ds(52 + 26 * f, 26)], co.at[f, :, pl.ds(at, G)]))
        early.append((rim0.at[pl.ds(104, 2)], inj.at[:, pl.ds(by8(spot(0, G, span)), G)]))
    else:
        before = chunks[k - 1]
        at = by8(spot(0, 2 * G, span) + G)
        at_before = spot(before - 2 * G, 2 * G, before)
        batches.append(level1_chunk(near_p, far_p, u1, at_before, at, 2 * G, even))
    early = sum((a for a, b in batches), early)
    late = sum((b for a, b in batches), [])
    copies = run_copies(early + late, sem)
    if last_slab:
        edge = spot(span - G, G, span)
        for ref in (u0, u1, co):
            for j in range(ref.shape[1]):
                ref[:, j, pl.ds(by8(edge + G), G)] = jnp.zeros((2, G, Z), F32)
        inj[:, pl.ds(edge, G)] = jnp.zeros((2, G, Z), F32)

    lane = lax.broadcasted_iota(jnp.int32, (span, Z), 1)
    first, last = lane == 0, lane == Z - 1
    y = slice(G, G + span)

    def second(row, carry):
        pull, gain, keep = coefficients(co[0, row, y], co[1, row, y])
        abc[0, row, y] = pull
        abc[1, row, y] = gain
        abc[2, row, y] = keep
        for f in range(2):
            centre, total = shifted(u1, f, row + 1, G, span, first, last)
            if f == 1:
                total += jnp.where(first, pltpu.roll(inj[0], 121 - row, 1), 0.0)
            u2[f, row, y] = keep * centre - pull * u0[f, row, y] + gain * total
        return carry

    base = jnp.where(even, 10, 2)
    wait_all(copies[: len(early)])
    lax.fori_loop(0, 14, lambda i, carry: second(base + i, carry), 0, unroll=14)
    wait_all(copies[len(early) :])

    def other_rows(i, carry):
        at_even = jnp.where(i < 10, i, i + 14)
        at_odd = jnp.where(i < 10, i + 16, i - 10)
        return second(jnp.where(even, at_even, at_odd), carry)

    lax.fori_loop(0, 12, other_rows, 0, unroll=12)
    levels = ((u0, 9), (u1, 10), (u2, 9), (u3, 8))
    low = spot((start if first_slab else start - G), size, Y)

    def finish(begin, length, sem_part):
        first_, last_ = first[:length], last[:length]
        lo = 2 * G + begin
        yy = slice(lo, lo + length)

        def third(row, carry):
            for f in range(2):
                centre, total = shifted(u2, f, row + 1, lo, length, first_, last_)
                if f == 1:
                    column = inj[1, G + begin : G + begin + length]
                    total += jnp.where(first_, pltpu.roll(column, 120 - row, 1), 0.0)
                u3[f, row, yy] = (
                    abc[2, row + 1, yy] * centre
                    - abc[0, row + 1, yy] * u1[f, row + 2, yy]
                    + abc[1, row + 1, yy] * total
                )
            return carry

        lax.fori_loop(0, 24, third, 0, unroll=24)

        def products(g, carry):
            cells = pl.ds(by8(lo + g * G), G)
            to = pl.ds(by8(begin + g * G), G)
            for parity in range(2):
                for tile in range(3):
                    rows_a = [-8 + parity + 8 * tile + 2 * j for j in range(4)]
                    held = [[ref[0, a + o, cells] for ref, o in levels] for a in rows_a]
                    for b in range(-8 + parity, 16, 2):
                        wanted = [
                            j for j, a in enumerate(rows_a) if 0 <= a + b < 16 and abs(b - a) <= 16
                        ]
                        if not wanted:
                            continue
                        right = [ref[1, b + o, cells] for ref, o in levels]
                        for j in wanted:
                            a = rows_a[j]
                            p = [l * r for l, r in zip(held[j], right)]
                            image[(b - a) // 2 + 8, (a + b) // 2, to] = (p[0] + p[1]) + (
                                p[2] + p[3]
                            )
            return carry

        lax.fori_loop(0, length // G, products, 0)
        copy = pltpu.make_async_copy(
            image.at[:, :, pl.ds(begin, length)],
            out_hbm.at[:, :, pl.ds(by8(low + begin), length)],
            sem_part,
        )
        copy.start()
        return copy

    groups = size // G
    cuts = [groups * j // PARTS * G for j in range(PARTS + 1)]
    wait_all(
        [finish(a, b - a, out_sem.at[j]) for j, (a, b) in enumerate(zip(cuts, cuts[1:]))]
    )


def call(kernel, outs, args, specs, scratch, name, out_specs=None, **extra):
    return pl.pallas_call(
        kernel,
        out_shape=[jax.ShapeDtypeStruct(s, F32) for s in outs],
        in_specs=specs,
        out_specs=out_specs or [HBM] * len(outs),
        scratch_shapes=scratch,
        compiler_params=pltpu.CompilerParams(vmem_limit_bytes=48 << 20),
        name=name,
        **extra,
    )(*args)


def after(value, *earlier):
    return lax.optimization_barrier((value, *earlier))[0]


def shards(fields_now, fields_later, velocity_term, damping, traces, receiver_live):
    count = lax.axis_size("gx")
    swap_x = [(i, i ^ 1) for i in range(count)]
    onward = [(i, i + 2) for i in range(0, count - 2, 2)]
    onward += [(i, i - 2) for i in range(3, count, 2)]
    backward = [(b, a) for a, b in onward]
    swap = [(0, 1), (1, 0)]
    dma = pltpu.SemaphoreType.DMA
    vm = pltpu.VMEM
    u0 = fields_now
    small = [vm((STEPS - 1, X, Y), F32), vm((X, Y), jnp.int32)]
    params = (u0, fields_later, velocity_term, damping, traces, receiver_live)
    u0, fields_later, velocity_term, damping, traces, receiver_live = (
        pltpu.with_memory_space_constraint(a, pltpu.HBM) for a in params
    )

    edge, brink = call(
        edge_kernel, [(2, 2, Y, Z), (2, X, G, Z)], (u0,), [HBM], [dma((3,))], "edge"
    )
    mine, rest, on0, back0 = call(
        prep_kernel,
        [(X, Y + G, Z), (2, 6, Y, Z), (4, Y + G, Z), (4, Y + G, Z)],
        (u0, velocity_term, damping, after(traces, brink), receiver_live),
        [HBM] * 5,
        [vm((2, X, Y), F32), *small, dma((8,)), dma((8,))],
        "prep",
    )
    near_edge = lax.ppermute(edge, "gx", swap_x)
    from_on0 = lax.ppermute(after(on0, near_edge), "gx", onward)
    beside = lax.ppermute(brink, "gy", swap)
    near_mine = lax.ppermute(mine, "gx", swap_x)
    far_edge = lax.ppermute(after(near_edge, beside), "gx", onward)
    near_rest = lax.ppermute(after(rest, near_edge, far_edge), "gx", swap_x)
    from_back0 = lax.ppermute(after(back0, near_rest), "gx", backward)

    u1, on1, brow, *parts = call(
        functools.partial(first_kernel, CHUNKS),
        [(2, X, Y, Z), (2, 2, Y, Z), (2, 2, Y, Z)] + [(2, 6, w, Z) for w in CHUNKS],
        (u0, fields_later, velocity_term, damping, near_edge, far_edge, beside, traces,
         receiver_live),
        [HBM] * 9,
        [
            vm((2, X + 2, Y + 2 * G, Z), F32),
            vm((2, X, Y, Z), F32),
            vm((X, Y, Z), F32),
            vm((X, Y, Z), F32),
            vm((2, X, Y, Z), F32),
            *small,
            dma((10 + len(CHUNKS),)),
            dma((2,)),
        ],
        "first",
    )
    far_mine = lax.ppermute(after(near_mine, u1, from_on0), "gx", onward)
    near_other = lax.ppermute(after(near_mine, u1, from_on0), "shot", swap)
    from_back1 = lax.ppermute(brow, "gx", backward)
    near_brow = lax.ppermute(after(brow, beside, near_mine), "gx", swap_x)
    near0 = lax.ppermute(after(parts[0], near_rest), "gx", swap_x)
    far_rest = lax.ppermute(after(near_rest, far_mine, from_back1), "gx", onward)
    from_on1 = lax.ppermute(after(on1, near_rest), "gx", onward)
    far_brow = lax.ppermute(after(from_back1, near_brow), "gx", swap_x)
    far_other = lax.ppermute(far_mine, "shot", swap)
    near1 = lax.ppermute(after(parts[1], near_other), "gx", swap_x)
    far0 = lax.ppermute(near0, "gx", onward)
    far1 = lax.ppermute(after(near1, from_on1, far_other), "gx", onward)
    near_chunks, far_chunks = [near0, near1], [far0, far1]

    base0 = (
        near_edge, near_rest, near_mine, near_other,
        far_edge, far_rest, far_mine, far_other,
        u0, velocity_term, damping, from_on0, from_back0,
    )
    base1 = (u1, from_on1, from_back1, near_brow, far_brow)
    rim0, columns = call(
        rim0_kernel,
        [(106, G, Z), (2, Y, Z)],
        (*base0, traces, receiver_live),
        [HBM] * (len(base0) + 2),
        [
            vm((2, 40, Y), F32),
            vm((2, 26, G, Z), F32),
            vm((2, 26, G, Z), F32),
            *small,
            dma((25,)),
            dma((2,)),
        ],
        "rim0",
        [VMEM, VMEM],
    )
    rim0 = lax.ppermute(rim0, "gy", swap)
    (rim1,) = call(
        functools.partial(rim1_kernel, CHUNKS[0]),
        [(2, 28, G, Z)],
        (*base1, near_chunks[0], far_chunks[0]),
        [HBM] * 7,
        [dma((7,))],
        "rim1",
        [VMEM],
    )
    rim1 = lax.ppermute(rim1, "gy", swap)

    image = None
    for k, width in enumerate(CHUNKS):
        first_slab, last_slab = k == 0, k == len(CHUNKS) - 1
        span = (G if first_slab else 2 * G) + width + (G if last_slab else 0)
        args = [*base0, *base1, columns, near_chunks[k], far_chunks[k]]
        if first_slab:
            args += [rim0, rim1]
        else:
            args += [near_chunks[k - 1], far_chunks[k - 1], image]
        wide = span + 2 * G
        (image,) = call(
            functools.partial(slab_kernel, k, CHUNKS),
            [(2 * LAG_HALF + 1, X, Y, Z)],
            args,
            [HBM] * len(args),
            [
                vm((2, 26, wide, Z), F32),
                vm((2, 28, wide, Z), F32),
                vm((2, 26, wide, Z), F32),
                vm((2, 24, wide, Z), F32),
                vm((2, 26, wide, Z), F32),
                vm((3, 26, wide, Z), F32),
                vm((2, span, Z), F32),
                vm((2 * LAG_HALF + 1, X, span - 2 * G, Z), F32),
                dma((32,)),
                dma((max(1, (span - 2 * G) // G),)),
            ],
            f"slab{k}",
            input_output_aliases={} if first_slab else {len(args) - 1: 0},
        )
    return image


def solution(mesh):
    placed = (
        P("shot", "gx", "gy", None),
        P("shot", "gx", "gy", None),
        P("gx", "gy", None),
        P("gx", "gy", None),
        P("shot", "gx", "gy"),
        P("gx", "gy"),
    )

    def body(fields_now, *others):
        fits = fields_now.shape == (2, X, 128, 128) and mesh.shape["gx"] % 2 == 0
        fits = fits and mesh.shape["gy"] == 2 and mesh.shape["shot"] == 2
        return (shards if fits else plain)(fields_now, *others)

    return jax.shard_map(
        body, mesh=mesh, in_specs=placed, out_specs=P("shot", "gx", "gy", None), check_vma=False
    )
```

```python
import functools
import jax
import jax.numpy as jnp
from jax import lax
from jax.experimental import pallas as pl
from jax.experimental.pallas import tpu as pltpu
from jax.sharding import PartitionSpec as P

STEPS = 4
LAG_HALF = 8
CHUNKS = (72, 56)


def padded(cells, sides, width):
    for axis, dim in sides:
        count = lax.axis_size(axis)
        ends = count - 1
        head = lax.slice_in_dim(cells, 0, width, axis=dim)
        tail = lax.slice_in_dim(cells, cells.shape[dim] - width, cells.shape[dim], axis=dim)
        cells = jnp.concatenate(
            [
                lax.ppermute(tail, axis, [(i, (i + 1) % count) for i in range(ends)]),
                cells,
                lax.ppermute(head, axis, [((i + 1) % count, i) for i in range(ends)]),
            ],
            axis=dim,
        )
    return cells


def lag_products(image_lags, slab, start, cells_x):
    updated = []
    for index, offset in enumerate(range(-LAG_HALF, LAG_HALF + 1)):
        left = slab[0, start - offset : start - offset + cells_x]
        right = slab[1, start + offset : start + offset + cells_x]
        updated.append(image_lags[index] + left * right)
    return updated


def source_mask(shape):
    channel_pick = (lax.broadcasted_iota(jnp.int32, shape, 0) == 1).astype(jnp.float32)
    surface = (lax.broadcasted_iota(jnp.int32, shape, 3) == 0).astype(jnp.float32)
    return channel_pick * surface


def plain(fields_now, fields_later, velocity_term, damping, traces, receiver_live):
    cells_x = fields_now.shape[1]
    live_mask = receiver_live.astype(jnp.float32)
    image_lags = [
        jnp.zeros(fields_now.shape[1:], jnp.float32) for offset in range(2 * LAG_HALF + 1)
    ]
    current = fields_now
    following = fields_later
    inject = source_mask(fields_now.shape)
    for time_step in range(STEPS):
        extended = padded(current, (("gx", 1),), LAG_HALF)
        image_lags = lag_products(image_lags, extended, LAG_HALF, cells_x)
        if time_step < STEPS - 1:
            crossed = padded(current, (("gy", 2),), 1)
            sum_x = (
                extended[:, LAG_HALF + 1 : LAG_HALF + 1 + cells_x]
                + extended[:, LAG_HALF - 1 : LAG_HALF - 1 + cells_x]
            )
            sum_y = crossed[:, :, 2:] + crossed[:, :, :-2]
            depth_pad = jnp.pad(current, ((0, 0), (0, 0), (0, 0), (1, 1)))
            sum_z = depth_pad[:, :, :, 2:] + depth_pad[:, :, :, :-2]
            source_plane = (live_mask * traces[time_step])[None, :, :, None]
            operated = sum_x + sum_y + sum_z - 6.0 * current + inject * source_plane
            earlier = (2.0 * current - (1.0 - damping) * following + velocity_term * operated) / (
                1.0 + damping
            )
            following = current
            current = earlier
    return jnp.stack(image_lags)


PARTS = 7
X = 8
Y = 128
Z = 128
G = 8
F32 = jnp.float32
HBM = pl.BlockSpec(memory_space=pltpu.HBM)
VMEM = pl.BlockSpec(memory_space=pltpu.VMEM)


def by8(value):
    return pl.multiple_of(value, G)


def place():
    even = lax.axis_index("gx") % 2 == 0
    return even, lax.axis_index("gy"), lax.axis_index("shot")


def run_copies(pieces, sem):
    copies = [pltpu.make_async_copy(a, b, sem.at[j]) for j, (a, b) in enumerate(pieces)]
    for c in copies:
        c.start()
    return copies


def wait_all(copies):
    for c in copies:
        c.wait()


def shifted(ref, f, row, lo, size, first, last):
    centre = ref[f, row, lo : lo + size]
    total = ref[f, row - 1, lo : lo + size] + ref[f, row + 1, lo : lo + size]
    total += ref[f, row, lo - 1 : lo - 1 + size] + ref[f, row, lo + 1 : lo + 1 + size]
    total += jnp.where(first, 0.0, pltpu.roll(centre, 1, 1))
    total += jnp.where(last, 0.0, pltpu.roll(centre, Z - 1, 1))
    return centre, total


def coefficients(vel, damp):
    inv = 1.0 / (1.0 + damp)
    gain = vel * inv
    return (1.0 - damp) * inv, gain, 2.0 * inv - 6.0 * gain


def receivers(traces_hbm, live_hbm, traces, live, sem):
    copies = run_copies([(traces_hbm, traces), (live_hbm, live)], sem)
    wait_all(copies)
    return live[...].astype(F32)


def edge_kernel(u0, edge, brink, sem):
    even, gy, shot = place()
    y = by8(jnp.where(gy == 0, Y - G, 0))
    pieces = [(u0.at[:, r], edge.at[:, e]) for e, r in ((0, 0), (1, X - 1))]
    pieces.append((u0.at[:, :, pl.ds(y, G)], brink))
    wait_all(run_copies(pieces, sem))


def prep_kernel(u0, v, d, traces_hbm, live_hbm, mine, rest, on0, back0, *scratch):
    t, traces, live, sem, sem2 = scratch
    even, gy, shot = place()
    own = pl.ds(0, Y)
    row = jnp.where(even, X - 1, 0)

    @pl.when(shot == 0)
    def _():
        pltpu.make_async_copy(v, mine.at[:, own], sem.at[7]).start()

    @pl.when(shot != 0)
    def _():
        pltpu.make_async_copy(d, mine.at[:, own], sem.at[7]).start()

    pieces = [(u0.at[:, pl.ds(1, 6)], rest)]
    for part, r in ((on0, row), (back0, X - 1 - row)):
        pieces.append((u0.at[:, r], part.at[pl.ds(0, 2), own]))
        pieces.append((v.at[r], part.at[2, own]))
        pieces.append((d.at[r], part.at[3, own]))
    copies = run_copies(pieces, sem)
    mask = receivers(traces_hbm, live_hbm, traces, live, sem2)
    for n in range(2):
        t[n] = mask * traces[n + 1]
    late = []
    for n in range(2):
        for k, part in enumerate((mine, on0, back0)):
            c = pltpu.make_async_copy(t.at[n], part.at[n, pl.ds(Y, G)], sem2.at[2 + 2 * k + n])
            c.start()
            late.append(c)
    wait_all(copies + late)
    pltpu.make_async_copy(v, mine.at[:, own], sem.at[7]).wait()


def surface_columns(rows):
    wide = jnp.concatenate([rows, jnp.zeros((Z - rows.shape[0], Y), F32)], 0)
    return wide.T


def first_kernel(chunks, *args):
    u0, later, v, d, near_e, far_e, beside, traces_hbm, live_hbm = args[:9]
    u1, on1, brow = args[9:12]
    parts = args[12 : 12 + len(chunks)]
    c, f0, vel, damp, out, traces, live, sem, sem2 = args[12 + len(chunks) :]
    even, gy, shot = place()
    own = pl.ds(0, Y)
    near_pick, near_row = jnp.where(even, 0, 1), jnp.where(even, 9, 0)
    far_pick, far_row = jnp.where(even, 1, 0), jnp.where(even, 0, 9)
    mid = pl.ds(G, Y)
    at = by8(jnp.where(gy == 0, Y + G, 0))
    copies = run_copies(
        [
            (u0, c.at[:, pl.ds(1, X), mid]),
            (near_e.at[:, near_pick], c.at[:, near_row, mid]),
            (far_e.at[:, far_pick], c.at[:, far_row, mid]),
            (beside, c.at[:, pl.ds(1, X), pl.ds(at, G)]),
            (later, f0),
            (v, vel),
            (d, damp),
        ],
        sem,
    )
    rim = by8(jnp.where(gy == 0, 0, Y + G))
    for f in range(2):
        for x in range(X):
            c[f, x + 1, pl.ds(rim, G)] = jnp.zeros((G, Z), F32)
    mask = receivers(traces_hbm, live_hbm, traces, live, sem2)
    column = surface_columns(mask * traces[0])
    wait_all(copies)
    lane = lax.broadcasted_iota(jnp.int32, (Y, Z), 1)
    first, last = lane == 0, lane == Z - 1
    for x in range(X):
        pull, gain, keep = coefficients(vel[x], damp[x])
        for f in range(2):
            centre, total = shifted(c, f, x + 1, G, Y, first, last)
            if f == 1:
                turned = pltpu.roll(column, Z - x, 1) if x else column
                total += jnp.where(first, turned, 0.0)
            out[f, x] = keep * centre - pull * f0[f, x] + gain * total
    row = jnp.where(even, 0, 6)
    pieces = [(out, u1), (out.at[:, pl.ds(6 - row, 2)], on1), (out.at[:, pl.ds(row, 2)], brow)]
    others = pl.ds(jnp.where(even, 2, 0), 6)
    begin = 0
    for width, part in zip(chunks, parts):
        y = by8(jnp.where(gy == 1, begin, Y - begin - width))
        pieces.append((out.at[:, others, pl.ds(y, width)], part))
        begin += width
    wait_all(run_copies(pieces, sem))


NAMES0 = ("ne", "nr", "na", "nb", "fe", "fr", "fa", "fb", "u0", "v", "d", "on", "back")
NAMES1 = ("u1", "on1", "back1", "nw", "fw")


def level0_pieces(refs, u0, co, src, dst, size, even, shot):
    near, far = jnp.where(even, 17, 1), jnp.where(even, 1, 17)
    s, d = pl.ds(src, size), pl.ds(dst, size)
    early, late = [], []
    for out, base, edge, rest, mine, other in (
        (early, near, refs["ne"], refs["nr"], refs["na"], refs["nb"]),
        (late, far, refs["fe"], refs["fr"], refs["fa"], refs["fb"]),
    ):
        out.append((edge.at[:, 0, s], u0(base, None, d)))
        out.append((edge.at[:, 1, s], u0(base + 7, None, d)))
        out.append((rest.at[:, :, s], u0(base + 1, 6, d)))
        out.append((mine.at[:, s], co(base, X, d, shot)))
        out.append((other.at[:, s], co(base, X, d, 1 - shot)))
    early.append((refs["u0"].at[:, :, s], u0(9, X, d)))
    early.append((refs["v"].at[:, s], co(9, X, d, 0)))
    early.append((refs["d"].at[:, s], co(9, X, d, 1)))
    for row, part in ((jnp.where(even, 0, 25), refs["on"]), (jnp.where(even, 25, 0), refs["back"])):
        late.append((part.at[pl.ds(0, 2), s], u0(row, None, d)))
        late.append((part.at[pl.ds(2, 2), s], co(row, None, d, None)))
    return early, late


def target(ref):
    def pick(row, rows, d, lead=None):
        lead = slice(None) if lead is None else lead
        return ref.at[lead, row if rows is None else pl.ds(row, rows), d]

    return pick


def level1_own(refs, u1, src, dst, size, even):
    s, d = pl.ds(src, size), pl.ds(dst, size)
    early = [(refs["u1"].at[:, :, s], u1.at[:, pl.ds(10, X), d])]
    late = []
    for out, part, at_even, at_odd in (
        (early, "nw", 24, 2), (late, "fw", 8, 18), (late, "on1", 0, 26), (late, "back1", 26, 0),
    ):
        row = jnp.where(even, at_even, at_odd)
        out.append((refs[part].at[:, :, s], u1.at[:, pl.ds(row, 2), d]))
    return early, late


def level1_chunk(near_ref, far_ref, u1, src, dst, size, even):
    near, far = jnp.where(even, 18, 4), jnp.where(even, 2, 20)
    s, d = pl.ds(src, size), pl.ds(dst, size)
    return (
        [(near_ref.at[:, :, s], u1.at[:, pl.ds(near, 6), d])],
        [(far_ref.at[:, :, s], u1.at[:, pl.ds(far, 6), d])],
    )


def rim0_kernel(*args):
    refs = dict(zip(NAMES0, args))
    traces_hbm, live_hbm, rim, columns, rows, u0, co, traces, live, sem, sem2 = args[len(NAMES0) :]
    even, gy, shot = place()
    y = by8(jnp.where(gy == 0, Y - G, 0))
    early, late = level0_pieces(refs, target(u0), target(co), y, 0, G, even, shot)
    pieces = early + late
    for part, at in (
        (refs["na"], jnp.where(even, 24, 8)),
        (refs["fa"], jnp.where(even, 8, 24)),
        (refs["on"], jnp.where(even, 0, 32)),
        (refs["back"], jnp.where(even, 32, 0)),
    ):
        for n in range(2):
            pieces.append((part.at[n, pl.ds(Y, G)], rows.at[n, pl.ds(by8(at), X)]))
    copies = run_copies(pieces, sem)
    mask = receivers(traces_hbm, live_hbm, traces, live, sem2)
    for n in range(2):
        rows[n, 16:24] = mask * traces[n + 1]
    wait_all(copies)
    for f in range(2):
        rim[26 * f : 26 * f + 26] = u0[f]
        rim[52 + 26 * f : 78 + 26 * f] = co[f]
    for n in range(2):
        columns[n] = surface_columns(rows[n])
        rim[104 + n] = columns[n, pl.ds(y, G)]


def rim1_kernel(chunk, *args):
    refs = dict(zip(NAMES1, args))
    near, far, out, sem = args[len(NAMES1) :]
    even, gy, shot = place()
    y = by8(jnp.where(gy == 0, Y - G, 0))
    yc = by8(jnp.where(gy == 0, chunk - G, 0))
    pieces = level1_own(refs, out, y, 0, G, even) + level1_chunk(near, far, out, yc, 0, G, even)
    wait_all(run_copies(sum(pieces, []), sem))


def slab_kernel(k, chunks, *args):
    n_in = len(NAMES0) + len(NAMES1)
    refs = dict(zip(NAMES0 + NAMES1, args[:n_in]))
    rest = list(args[n_in:])
    columns = rest.pop(0)
    near_k, far_k = rest.pop(0), rest.pop(0)
    first_slab, last_slab = k == 0, k == len(chunks) - 1
    if first_slab:
        rim0, rim1 = rest.pop(0), rest.pop(0)
    else:
        near_p, far_p, _ = rest.pop(0), rest.pop(0), rest.pop(0)
    out_hbm, u0, u1, u2, u3, co, abc, inj, image, sem, out_sem = rest
    even, gy, shot = place()
    start, width = sum(chunks[:k]), chunks[k]
    lead = G if first_slab else 2 * G
    span = lead + width + (G if last_slab else 0)
    size = span - 2 * G

    def spot(at, length, total):
        return by8(jnp.where(gy == 1, at, total - at - length))

    ahead = 0 if first_slab else 2 * G
    src = spot(start - ahead, ahead + width, Y)
    here = spot(lead - ahead, ahead + width, span)
    dst = by8(here + G)
    batches = [
        level0_pieces(refs, target(u0), target(co), src, dst, ahead + width, even, shot),
        level1_own(refs, u1, src, dst, ahead + width, even),
    ]
    at = by8(spot(lead, width, span) + G)
    batches.append(level1_chunk(near_k, far_k, u1, 0, at, width, even))
    early = [(columns.at[:, pl.ds(src, ahead + width)], inj.at[:, pl.ds(here, ahead + width)])]
    if first_slab:
        at = by8(spot(0, G, span) + G)
        early.append((rim1, u1.at[:, :, pl.ds(at, G)]))
        for f in range(2):
            early.append((rim0.at[pl.ds(26 * f, 26)], u0.at[f, :, pl.ds(at, G)]))
            early.append((rim0.at[pl.ds(52 + 26 * f, 26)], co.at[f, :, pl.ds(at, G)]))
        early.append((rim0.at[pl.ds(104, 2)], inj.at[:, pl.ds(by8(spot(0, G, span)), G)]))
    else:
        before = chunks[k - 1]
        at = by8(spot(0, 2 * G, span) + G)
        at_before = spot(before - 2 * G, 2 * G, before)
        batches.append(level1_chunk(near_p, far_p, u1, at_before, at, 2 * G, even))
    early = sum((a for a, b in batches), early)
    late = sum((b for a, b in batches), [])
    copies = run_copies(early + late, sem)
    if last_slab:
        edge = spot(span - G, G, span)
        for ref in (u0, u1, co):
            for j in range(ref.shape[1]):
                ref[:, j, pl.ds(by8(edge + G), G)] = jnp.zeros((2, G, Z), F32)
        inj[:, pl.ds(edge, G)] = jnp.zeros((2, G, Z), F32)

    lane = lax.broadcasted_iota(jnp.int32, (span, Z), 1)
    first, last = lane == 0, lane == Z - 1
    y = slice(G, G + span)

    def second(row, carry):
        pull, gain, keep = coefficients(co[0, row, y], co[1, row, y])
        abc[0, row, y] = pull
        abc[1, row, y] = gain
        abc[2, row, y] = keep
        for f in range(2):
            centre, total = shifted(u1, f, row + 1, G, span, first, last)
            if f == 1:
                total += jnp.where(first, pltpu.roll(inj[0], 121 - row, 1), 0.0)
            u2[f, row, y] = keep * centre - pull * u0[f, row, y] + gain * total
        return carry

    base = jnp.where(even, 10, 2)
    wait_all(copies[: len(early)])
    lax.fori_loop(0, 14, lambda i, carry: second(base + i, carry), 0, unroll=14)
    wait_all(copies[len(early) :])

    def other_rows(i, carry):
        at_even = jnp.where(i < 10, i, i + 14)
        at_odd = jnp.where(i < 10, i + 16, i - 10)
        return second(jnp.where(even, at_even, at_odd), carry)

    lax.fori_loop(0, 12, other_rows, 0, unroll=12)
    levels = ((u0, 9), (u1, 10), (u2, 9), (u3, 8))
    low = spot((start if first_slab else start - G), size, Y)

    def finish(begin, length, sem_part):
        first_, last_ = first[:length], last[:length]
        lo = 2 * G + begin
        yy = slice(lo, lo + length)

        def third(row, carry):
            for f in range(2):
                centre, total = shifted(u2, f, row + 1, lo, length, first_, last_)
                if f == 1:
                    column = inj[1, G + begin : G + begin + length]
                    total += jnp.where(first_, pltpu.roll(column, 120 - row, 1), 0.0)
                u3[f, row, yy] = (
                    abc[2, row + 1, yy] * centre
                    - abc[0, row + 1, yy] * u1[f, row + 2, yy]
                    + abc[1, row + 1, yy] * total
                )
            return carry

        lax.fori_loop(0, 24, third, 0, unroll=24)

        def products(g, carry):
            cells = pl.ds(by8(lo + g * G), G)
            to = pl.ds(by8(begin + g * G), G)
            for parity in range(2):
                for tile in range(3):
                    rows_a = [-8 + parity + 8 * tile + 2 * j for j in range(4)]
                    held = [[ref[0, a + o, cells] for ref, o in levels] for a in rows_a]
                    for b in range(-8 + parity, 16, 2):
                        wanted = [
                            j for j, a in enumerate(rows_a) if 0 <= a + b < 16 and abs(b - a) <= 16
                        ]
                        if not wanted:
                            continue
                        right = [ref[1, b + o, cells] for ref, o in levels]
                        for j in wanted:
                            a = rows_a[j]
                            p = [l * r for l, r in zip(held[j], right)]
                            image[(b - a) // 2 + 8, (a + b) // 2, to] = (p[0] + p[1]) + (
                                p[2] + p[3]
                            )
            return carry

        lax.fori_loop(0, length // G, products, 0)
        copy = pltpu.make_async_copy(
            image.at[:, :, pl.ds(begin, length)],
            out_hbm.at[:, :, pl.ds(by8(low + begin), length)],
            sem_part,
        )
        copy.start()
        return copy

    groups = size // G
    cuts = [groups * j // PARTS * G for j in range(PARTS + 1)]
    wait_all(
        [finish(a, b - a, out_sem.at[j]) for j, (a, b) in enumerate(zip(cuts, cuts[1:]))]
    )


def call(kernel, outs, args, specs, scratch, name, out_specs=None, **extra):
    return pl.pallas_call(
        kernel,
        out_shape=[jax.ShapeDtypeStruct(s, F32) for s in outs],
        in_specs=specs,
        out_specs=out_specs or [HBM] * len(outs),
        scratch_shapes=scratch,
        compiler_params=pltpu.CompilerParams(vmem_limit_bytes=48 << 20),
        name=name,
        **extra,
    )(*args)


def after(value, *earlier):
    return lax.optimization_barrier((value, *earlier))[0]


def shards(fields_now, fields_later, velocity_term, damping, traces, receiver_live):
    count = lax.axis_size("gx")
    swap_x = [(i, i ^ 1) for i in range(count)]
    onward = [(i, i + 2) for i in range(0, count - 2, 2)]
    onward += [(i, i - 2) for i in range(3, count, 2)]
    backward = [(b, a) for a, b in onward]
    swap = [(0, 1), (1, 0)]
    dma = pltpu.SemaphoreType.DMA
    vm = pltpu.VMEM
    u0 = fields_now
    small = [vm((STEPS - 1, X, Y), F32), vm((X, Y), jnp.int32)]
    params = (u0, fields_later, velocity_term, damping, traces, receiver_live)
    u0, fields_later, velocity_term, damping, traces, receiver_live = (
        pltpu.with_memory_space_constraint(a, pltpu.HBM) for a in params
    )

    edge, brink = call(
        edge_kernel, [(2, 2, Y, Z), (2, X, G, Z)], (u0,), [HBM], [dma((3,))], "edge"
    )
    mine, rest, on0, back0 = call(
        prep_kernel,
        [(X, Y + G, Z), (2, 6, Y, Z), (4, Y + G, Z), (4, Y + G, Z)],
        (u0, velocity_term, damping, after(traces, brink), receiver_live),
        [HBM] * 5,
        [vm((2, X, Y), F32), *small, dma((8,)), dma((8,))],
        "prep",
    )
    near_edge = lax.ppermute(edge, "gx", swap_x)
    from_on0 = lax.ppermute(after(on0, near_edge), "gx", onward)
    beside = lax.ppermute(brink, "gy", swap)
    near_mine = lax.ppermute(mine, "gx", swap_x)
    far_edge = lax.ppermute(after(near_edge, beside), "gx", onward)
    near_rest = lax.ppermute(after(rest, near_edge, far_edge), "gx", swap_x)
    from_back0 = lax.ppermute(after(back0, near_rest), "gx", backward)

    u1, on1, brow, *parts = call(
        functools.partial(first_kernel, CHUNKS),
        [(2, X, Y, Z), (2, 2, Y, Z), (2, 2, Y, Z)] + [(2, 6, w, Z) for w in CHUNKS],
        (u0, fields_later, velocity_term, damping, near_edge, far_edge, beside, traces,
         receiver_live),
        [HBM] * 9,
        [
            vm((2, X + 2, Y + 2 * G, Z), F32),
            vm((2, X, Y, Z), F32),
            vm((X, Y, Z), F32),
            vm((X, Y, Z), F32),
            vm((2, X, Y, Z), F32),
            *small,
            dma((10 + len(CHUNKS),)),
            dma((2,)),
        ],
        "first",
    )
    far_mine = lax.ppermute(after(near_mine, u1, from_on0), "gx", onward)
    near_other = lax.ppermute(after(near_mine, u1, from_on0), "shot", swap)
    from_back1 = lax.ppermute(brow, "gx", backward)
    near_brow = lax.ppermute(after(brow, beside, near_mine), "gx", swap_x)
    near0 = lax.ppermute(after(parts[0], near_rest), "gx", swap_x)
    far_rest = lax.ppermute(after(near_rest, far_mine, from_back1), "gx", onward)
    from_on1 = lax.ppermute(after(on1, near_rest), "gx", onward)
    far_brow = lax.ppermute(after(from_back1, near_brow), "gx", swap_x)
    far_other = lax.ppermute(far_mine, "shot", swap)
    near1 = lax.ppermute(after(parts[1], near_other), "gx", swap_x)
    far0 = lax.ppermute(near0, "gx", onward)
    far1 = lax.ppermute(after(near1, from_on1, far_other), "gx", onward)
    near_chunks, far_chunks = [near0, near1], [far0, far1]

    base0 = (
        near_edge, near_rest, near_mine, near_other,
        far_edge, far_rest, far_mine, far_other,
        u0, velocity_term, damping, from_on0, from_back0,
    )
    base1 = (u1, from_on1, from_back1, near_brow, far_brow)
    rim0, columns = call(
        rim0_kernel,
        [(106, G, Z), (2, Y, Z)],
        (*base0, traces, receiver_live),
        [HBM] * (len(base0) + 2),
        [
            vm((2, 40, Y), F32),
            vm((2, 26, G, Z), F32),
            vm((2, 26, G, Z), F32),
            *small,
            dma((25,)),
            dma((2,)),
        ],
        "rim0",
        [VMEM, VMEM],
    )
    rim0 = lax.ppermute(rim0, "gy", swap)
    (rim1,) = call(
        functools.partial(rim1_kernel, CHUNKS[0]),
        [(2, 28, G, Z)],
        (*base1, near_chunks[0], far_chunks[0]),
        [HBM] * 7,
        [dma((7,))],
        "rim1",
        [VMEM],
    )
    rim1 = lax.ppermute(rim1, "gy", swap)

    image = None
    for k, width in enumerate(CHUNKS):
        first_slab, last_slab = k == 0, k == len(CHUNKS) - 1
        span = (G if first_slab else 2 * G) + width + (G if last_slab else 0)
        args = [*base0, *base1, columns, near_chunks[k], far_chunks[k]]
        if first_slab:
            args += [rim0, rim1]
        else:
            args += [near_chunks[k - 1], far_chunks[k - 1], image]
        wide = span + 2 * G
        (image,) = call(
            functools.partial(slab_kernel, k, CHUNKS),
            [(2 * LAG_HALF + 1, X, Y, Z)],
            args,
            [HBM] * len(args),
            [
                vm((2, 26, wide, Z), F32),
                vm((2, 28, wide, Z), F32),
                vm((2, 26, wide, Z), F32),
                vm((2, 24, wide, Z), F32),
                vm((2, 26, wide, Z), F32),
                vm((3, 26, wide, Z), F32),
                vm((2, span, Z), F32),
                vm((2 * LAG_HALF + 1, X, span - 2 * G, Z), F32),
                dma((32,)),
                dma((max(1, (span - 2 * G) // G),)),
            ],
            f"slab{k}",
            input_output_aliases={} if first_slab else {len(args) - 1: 0},
        )
    return image


def solution(mesh):
    placed = (
        P("shot", "gx", "gy", None),
        P("shot", "gx", "gy", None),
        P("gx", "gy", None),
        P("gx", "gy", None),
        P("shot", "gx", "gy"),
        P("gx", "gy"),
    )

    def body(fields_now, *others):
        fits = fields_now.shape == (2, X, 128, 128) and mesh.shape["gx"] % 2 == 0
        fits = fits and mesh.shape["gy"] == 2 and mesh.shape["shot"] == 2
        return (shards if fits else plain)(fields_now, *others)

    return jax.shard_map(
        body, mesh=mesh, in_specs=placed, out_specs=P("shot", "gx", "gy", None), check_vma=False
    )
```
